512 devices in a mesh: ctx: 16 (over y, z_hi, core), row: 4 (over x), col: 8 (over z_lo).
Axes of the slice: x: 4, y: 4, z: 16 (z_hi: 2, z_lo: 8; z = z_hi * 8 + z_lo), core: 2. Of those that a mesh axis runs over, the one named last changes fastest.
Arguments:
- patches: bfloat16 [12288, 2048], P(('ctx', 'row'), 'col'), may hold values from -6 to 6
- visible: int32 [12288], P(('ctx', 'row')), may hold values from -1 to 262143, as said below
- ln_gain: float32 [2048], replicated, may hold values from 0.1 to 1.9
- ln_bias: float32 [2048], replicated, may hold values from -3 to 3
- w_query: bfloat16 [2048, 2048], P('row', 'col')
- w_key: bfloat16 [2048, 2048], P('row', 'col')
- w_value: bfloat16 [2048, 2048], P('row', 'col'), may hold values from -0.125 to 0.125
- w_output: bfloat16 [2048, 2048], P('row', 'col'), may hold values from -0.375 to 0.375
Outputs:
- attn_out: float32 [12288, 2048], P(('ctx', 'row'), 'col')
The draws below stay inside these ranges and needn't reach their ends.
Inputs may be any that keep to these rules, and one draw needn't show every extreme that they name: Slots s * 768 to (s + 1) * 768 - 1 form slab s: first the distinct visible patch numbers of that slab in increasing order, all in s * 16384 to (s + 1) * 16384 - 1, then -1 in every remaining slot. Each slab holds 384 or more visible patches, and some slab is full.
All inputs are finite; a program needn't handle non-finite values.
Results may differ from the reference program's by a relative error of at most 0.0094.
Values may be sent and summed in bfloat16 or wider, within the bound.
No kernel may reach another device: no remote copies, remote signals or barrier semaphores. Data moves between devices by JAX's collectives and lax.ppermute only.
A program may use at most 128 MiB of HBM per device.

```python
import math
import jax
import jax.numpy as jnp
from jax import lax

D = 2048
HEADS = 16
HEAD_DIM = 128
GRID = 64
TOK_CTX = 768
TOKENS = 12288
REGION = 16384


def draw_visible(key, part):
    slab_count = TOKENS // TOK_CTX
    full_key, count_key, perm_key = jax.random.split(key, 3)
    full_slab = jax.random.randint(full_key, (), 0, slab_count)
    counts = TOK_CTX - jax.random.randint(count_key, (slab_count,), 0, TOK_CTX // 2 + 1)
    slab_ids = jnp.arange(slab_count, dtype=jnp.int32)
    counts = jnp.where(slab_ids == full_slab, TOK_CTX, counts)

    def one_slab(slab):
        chosen = jax.random.permutation(jax.random.fold_in(perm_key, slab), REGION)[:TOK_CTX]
        return jnp.sort(chosen).astype(jnp.int32) + slab * REGION
    picks = jax.vmap(one_slab)(slab_ids)
    slots = jnp.arange(TOK_CTX, dtype=jnp.int32)
    result = jnp.where(slots[None, :] < counts[:, None], picks, -1)
    return result.reshape(TOKENS).astype(jnp.int32)


def shared_base(key):
    return jax.random.normal(jax.random.fold_in(key, 7), (D, D), jnp.float32) / math.sqrt(D)


def draw_w_query(key, part):
    base = shared_base(key)
    return (2.0 * base).astype(jnp.bfloat16)


def draw_w_key(key, part):
    other = jax.random.normal(jax.random.fold_in(key, 11), (D, D), jnp.float32) / math.sqrt(D)
    return other.astype(jnp.bfloat16)


def levels(stream_key, extent, cuts, low, largest):
    def one(axis_at, blocks):
        heights = jax.random.uniform(jax.random.fold_in(jax.random.fold_in(stream_key, 6), axis_at), (blocks,), jnp.float32, low / len(cuts), largest / len(cuts))
        return jnp.repeat(jnp.exp(heights), extent[axis_at] // blocks).reshape((-1,) + (1,) * (len(extent) - axis_at - 1))

    gain = one(*cuts[0])
    for cut in cuts[1:]:
        gain = gain * one(*cut)
    return gain


def noise(key, extent, width, limit, shards=(), kind=jnp.bfloat16):
    entries = jax.random.normal(key, extent, jnp.float32) * width
    if len(shards) > 0:
        entries = levels(key, extent, shards, -0.22, 0.18) * entries
    return jnp.clip(entries, min=-limit, max=limit).astype(kind)


def setup_inputs(seed: int = 0) -> dict:
    streams_of = jax.random.split(jax.random.key(seed), 9)
    patches = noise(streams_of[0], (TOKENS, D), 1.0, 6.0, ((0, 64), (1, 8)))
    visible = draw_visible(jax.random.fold_in(streams_of[8], 71), 0)
    ln_gain = jnp.clip(1.0 + 0.18 * jax.random.normal(streams_of[2], (D,), jnp.float32), 0.1, 1.9)
    ln_bias = noise(streams_of[3], (D,), 0.5, 3.0, (), jnp.float32)
    w_query = draw_w_query(jax.random.fold_in(streams_of[8], 71), 0)
    w_key = draw_w_key(jax.random.fold_in(streams_of[8], 71), 0)
    w_value = noise(streams_of[6], (D, D), D ** -0.5, 0.125, ((0, 4), (1, 8)))
    w_output = noise(streams_of[7], (D, D), (D // 8) ** -0.5, 0.375, ((0, 4), (1, 8)))
    return dict(patches=patches, visible=visible, ln_gain=ln_gain, ln_bias=ln_bias, w_query=w_query, w_key=w_key, w_value=w_value, w_output=w_output)


def embed(visible, full_width):
    patch_id = jnp.maximum(visible, 0)
    plane_size = GRID * GRID
    coord_x = (patch_id // plane_size).astype(jnp.float32)
    coord_y = (patch_id // GRID % GRID).astype(jnp.float32)
    coord_z = (patch_id % GRID).astype(jnp.float32)
    channel = jnp.arange(full_width, dtype=jnp.int32)
    axis_pick = channel % 3
    frequency = jnp.exp(-math.log(10000.0) * (channel // 6 * 6).astype(jnp.float32) / full_width)
    offset_phase = 0.5 * math.pi * (channel // 3 % 2).astype(jnp.float32)
    picked = jnp.where(axis_pick[None, :] == 0, coord_x[:, None], jnp.where(axis_pick[None, :] == 1, coord_y[:, None], coord_z[:, None]))
    return jnp.sin(picked * frequency[None, :] + offset_phase[None, :])

def normalize(hidden, ln_gain, ln_bias):
    center = hidden - lax.optimization_barrier(jnp.mean(hidden, axis=1, keepdims=True))
    spread = lax.optimization_barrier(jnp.mean(center * center, axis=1, keepdims=True))
    return (center * lax.rsqrt(spread + 1e-06) * ln_gain[None, :] + ln_bias[None, :]).astype(jnp.bfloat16)

def reference(patches, visible, ln_gain, ln_bias, w_query, w_key, w_value, w_output):
    hidden = patches.astype(jnp.float32) + embed(visible, D)
    normed = normalize(hidden, ln_gain, ln_bias)
    query_f = jnp.dot(normed, w_query, preferred_element_type=jnp.float32)
    query = (query_f * (1.0 / math.sqrt(HEAD_DIM))).astype(jnp.bfloat16)
    keys = jnp.dot(normed, w_key, preferred_element_type=jnp.float32).astype(jnp.bfloat16)
    values = jnp.dot(normed, w_value, preferred_element_type=jnp.float32).astype(jnp.bfloat16)
    live = visible >= 0
    query_h = query.reshape(TOKENS, HEADS, HEAD_DIM).transpose(1, 0, 2)
    keys_h = keys.reshape(TOKENS, HEADS, HEAD_DIM).transpose(1, 0, 2)
    values_h = values.reshape(TOKENS, HEADS, HEAD_DIM).transpose(1, 0, 2)

    def one_head(parts):
        q_part, k_part, v_part = parts
        scores = jnp.dot(q_part, k_part.T, preferred_element_type=jnp.float32)
        scores = jnp.where(live[None, :], scores, -1e+30)
        top_score = lax.optimization_barrier(jnp.max(scores, axis=1, keepdims=True))
        weights = jnp.exp(scores - top_score)
        totals = lax.optimization_barrier(jnp.sum(weights, axis=1, keepdims=True))
        accum = jnp.dot(weights.astype(jnp.bfloat16), v_part, preferred_element_type=jnp.float32)
        return accum / totals
    mixed = lax.map(one_head, (query_h, keys_h, values_h))
    mixed = mixed.transpose(1, 0, 2).reshape(TOKENS, D).astype(jnp.bfloat16)
    return jnp.dot(mixed, w_output, preferred_element_type=jnp.float32)
```

```python
import math

import jax
import jax.numpy as jnp
from jax import lax
from jax.experimental import pallas as pl
from jax.experimental.pallas import tpu as pltpu
from jax.sharding import Mesh
from jax.sharding import PartitionSpec as P

HEAD_DIM = 128
GRID = 64
ROWS = 192
F32 = jnp.float32
BF16 = jnp.bfloat16
SHIFTS = (0, 1, 3, 2)


def embed(visible, full_width):
    patch_id = jnp.maximum(visible, 0)
    plane_size = GRID * GRID
    coord_x = (patch_id // plane_size).astype(F32)
    coord_y = (patch_id // GRID % GRID).astype(F32)
    coord_z = (patch_id % GRID).astype(F32)
    channel = jnp.arange(full_width, dtype=jnp.int32)
    axis_pick = channel % 3
    frequency = jnp.exp(-math.log(10000.0) * (channel // 6 * 6).astype(F32) / full_width)
    offset_phase = 0.5 * math.pi * (channel // 3 % 2).astype(F32)
    picked = jnp.where(
        axis_pick[None, :] == 0,
        coord_x[:, None],
        jnp.where(axis_pick[None, :] == 1, coord_y[:, None], coord_z[:, None]),
    )
    return jnp.sin(picked * frequency[None, :] + offset_phase[None, :])


def spread(block, axes, count):
    copies = jnp.broadcast_to(block[None], (count,) + block.shape)
    return lax.all_to_all(copies, axes, 0, 0)


def ring(count, shift):
    return [(i, (i + shift) % count) for i in range(count)]


def norm_kernel(g_ref, pos_ref, gain_ref, bias_ref, out_ref):
    step = 64
    for r in range(0, ROWS, step):
        parts = [
            g_ref[z, r : r + step, :].astype(F32) + pos_ref[r : r + step, z * 256 : (z + 1) * 256]
            for z in range(8)
        ]
        total = sum(jnp.sum(p, axis=1, keepdims=True) for p in parts)
        mean = total * (1.0 / 2048)
        parts = [p - mean for p in parts]
        square = sum(jnp.sum(p * p, axis=1, keepdims=True) for p in parts)
        scale = lax.rsqrt(square * (1.0 / 2048) + 1e-06)
        for z in range(8):
            lanes = slice(z * 256, (z + 1) * 256)
            value = parts[z] * scale * gain_ref[:, lanes] + bias_ref[:, lanes]
            out_ref[z // 2, r : r + step, (z % 2) * 256 : (z % 2 + 1) * 256] = value.astype(BF16)


def qkv_kernel(src_ref, n_ref, w0_ref, w1_ref, w2_ref, w3_ref, cnt_ref, q_ref, kv_ref):
    for c in range(2):
        acc = jnp.zeros((ROWS, 384), F32)
        for s, w_ref in enumerate((w0_ref, w1_ref, w2_ref, w3_ref)):
            acc = acc + jnp.dot(
                n_ref[c, src_ref[s]], w_ref[:, :384], preferred_element_type=F32
            )
        rows = slice(c * ROWS, (c + 1) * ROWS)
        q_ref[rows, :] = (acc[:, :128] * (1.0 / math.sqrt(HEAD_DIM))).astype(BF16)
        kv_ref[rows, :] = acc[:, 128:384].astype(BF16)
    kv_ref[2 * ROWS : 2 * ROWS + 16, :] = cnt_ref[...].reshape(16, 256).astype(BF16)


def attn_kernel(q_ref, kv_ref, out_ref, s_ref, acc_ref):
    width = q_ref.shape[0]
    blocks = kv_ref.shape[0]
    query = q_ref[...]
    nt = (((1,), (1,)), ((), ()))
    tn = (((0,), (0,)), ((), ()))

    def first(b, best):
        for c in range(2):
            keys = kv_ref[b, c * ROWS : (c + 1) * ROWS, :128]
            score = lax.dot_general(keys, query, nt, preferred_element_type=F32)
            row = lax.broadcasted_iota(jnp.int32, (ROWS, width), 0).astype(F32)
            live = kv_ref[b, pl.ds(2 * ROWS + 8 * c, 1), :].astype(F32)
            live = jnp.concatenate([live] * (width // 256), axis=1)
            score = jnp.where(row < live, score, -1e30)
            s_ref[pl.ds(b * 2 * ROWS + c * ROWS, ROWS), :] = score
            best = jnp.maximum(best, jnp.max(score, axis=0, keepdims=True))
        return best

    best = lax.fori_loop(0, blocks, first, jnp.full((1, width), -1e30, F32))
    acc_ref[...] = jnp.zeros_like(acc_ref)

    def second(b, total):
        weight = jnp.exp(s_ref[pl.ds(b * 2 * ROWS, 2 * ROWS), :] - best)
        total = total + jnp.sum(weight, axis=0, keepdims=True)
        values = kv_ref[b, : 2 * ROWS, 128:256]
        acc_ref[...] += lax.dot_general(
            values, weight.astype(BF16), tn, preferred_element_type=F32
        )
        return total

    total = lax.fori_loop(0, blocks, second, jnp.zeros((1, width), F32))
    mixed = (acc_ref[...] / total).T.astype(BF16)
    level = best + jnp.log(total)
    high = level.astype(BF16)
    rest = level - high.astype(F32)
    mid = rest.astype(BF16)
    low = (rest - mid.astype(F32)).astype(BF16)
    for x in range(width // (2 * ROWS)):
        stats = []
        for part in (high, mid, low):
            for piece in range(3):
                at = x * 2 * ROWS + piece * 128
                stats.append(part[:, at : at + 128].astype(F32))
        stats.append(jnp.zeros((7, 128), F32))
        stats = jnp.concatenate(stats, axis=0).astype(BF16)
        for c in range(2):
            at = (2 * x + c) * ROWS
            out_ref[2 * x + c, :ROWS, :] = mixed[at : at + ROWS, :]
            out_ref[2 * x + c, ROWS : ROWS + 16, :] = stats


def out_kernel(src_ref, m_ref, w0_ref, w1_ref, w2_ref, w3_ref, out_ref):
    acc = jnp.zeros(out_ref.shape, F32)
    for s, w_ref in enumerate((w0_ref, w1_ref, w2_ref, w3_ref)):
        for half in range(2):
            acc = acc + jnp.dot(
                m_ref[2 * src_ref[s] + half],
                w_ref[half * 256 : (half + 1) * 256, 384:640],
                preferred_element_type=F32,
            )
    out_ref[...] = acc


VMEM = pl.BlockSpec(memory_space=pltpu.VMEM)
SMEM = pl.BlockSpec(memory_space=pltpu.SMEM)
PARAMS = pltpu.CompilerParams(vmem_limit_bytes=48 * 1024 * 1024)


def body(patches, visible, ln_gain, ln_bias, w_query, w_key, w_value, w_output):
    core = lax.axis_index("core")
    row = lax.axis_index("row")
    lane = core * HEAD_DIM
    w_own = jnp.concatenate(
        [lax.dynamic_slice_in_dim(w, lane, HEAD_DIM, 1) for w in (w_query, w_key, w_value)]
        + [w_output],
        axis=1,
    )
    weights = [w_own] + [lax.ppermute(w_own, "row", ring(4, s)) for s in SHIFTS[1:]]
    source = jnp.stack([(row - s) % 4 for s in SHIFTS]).astype(jnp.int32)

    live = jnp.sum((visible >= 0).astype(F32))
    own = jnp.full((8, 256), live, F32)
    other = lax.ppermute(own, "core", ring(2, 1))
    counts = jnp.where(core == 0, jnp.stack([own, other]), jnp.stack([other, own]))

    pos = embed(visible, 2048)
    gathered = spread(patches, "col", 8)
    normed = pl.pallas_call(
        norm_kernel,
        out_shape=jax.ShapeDtypeStruct((4, ROWS, 512), BF16),
        in_specs=[VMEM] * 4,
        out_specs=VMEM,
        compiler_params=PARAMS,
        name="norm",
    )(gathered, pos, ln_gain[None, :], ln_bias[None, :])
    normed = spread(normed, "core", 2)
    query, kv = pl.pallas_call(
        qkv_kernel,
        out_shape=(
            jax.ShapeDtypeStruct((2 * ROWS, 128), BF16),
            jax.ShapeDtypeStruct((2 * ROWS + 16, 256), BF16),
        ),
        in_specs=[SMEM] + [VMEM] * 6,
        out_specs=(VMEM, VMEM),
        compiler_params=PARAMS,
        name="qkv",
    )(source, normed, *weights, counts)
    far = lax.ppermute(kv, ("zh", "col"), ring(16, 8))
    query = spread(query, "row", 4).reshape(8 * ROWS, 128)
    kv = spread(jnp.stack([kv, far]), "y", 4).reshape(8, 2 * ROWS + 16, 256)
    part = pl.pallas_call(
        attn_kernel,
        grid=(2,),
        out_shape=jax.ShapeDtypeStruct((8, ROWS + 16, 128), BF16),
        in_specs=[
            pl.BlockSpec((4 * ROWS, 128), lambda i: (i, 0)),
            pl.BlockSpec((8, 2 * ROWS + 16, 256), lambda i: (0, 0, 0)),
        ],
        out_specs=pl.BlockSpec((4, ROWS + 16, 128), lambda i: (i, 0, 0)),
        scratch_shapes=[
            pltpu.VMEM((16 * ROWS, 4 * ROWS), F32),
            pltpu.VMEM((128, 4 * ROWS), F32),
        ],
        compiler_params=PARAMS,
        name="attn",
    )(query, kv)
    part = lax.all_to_all(part, ("row", "core"), 0, 0).reshape(4, 2, ROWS + 16, 128)
    stats = part[:, :, ROWS : ROWS + 9, :].astype(F32).reshape(4, 2, 3, 2 * ROWS).sum(axis=2)
    stats = lax.dynamic_slice_in_dim(stats, core * ROWS, ROWS, 2)
    share = jnp.exp(stats - jnp.max(stats, axis=0, keepdims=True))
    share = share / jnp.sum(share, axis=0, keepdims=True)
    mixed = jnp.sum(part[:, :, :ROWS, :].astype(F32) * share[..., None], axis=0)
    mixed = jnp.concatenate([mixed[0], mixed[1]], axis=1).astype(BF16)
    mixed = spread(mixed, "col", 8)
    return pl.pallas_call(
        out_kernel,
        out_shape=jax.ShapeDtypeStruct((ROWS, 256), F32),
        in_specs=[SMEM] + [VMEM] * 5,
        out_specs=VMEM,
        compiler_params=PARAMS,
        name="out",
    )(source, mixed, *weights)


def solution(mesh):
    fine = Mesh(mesh.devices.reshape(4, 2, 2, 4, 8), ("y", "zh", "core", "row", "col"))
    tokens = ("y", "zh", "core", "row")
    placed = (
        P(tokens, "col"),
        P(tokens),
        P(),
        P(),
        P("row", "col"),
        P("row", "col"),
        P("row", "col"),
        P("row", "col"),
    )
    return jax.shard_map(
        body, mesh=fine, in_specs=placed, out_specs=P(tokens, "col"), check_vma=False
    )
```

```python
import math

import jax
import jax.numpy as jnp
from jax import lax
from jax.experimental import pallas as pl
from jax.experimental.pallas import tpu as pltpu
from jax.sharding import Mesh
from jax.sharding import PartitionSpec as P


HEAD_DIM = 128
GRID = 64
ROWS = 192
F32 = jnp.float32
BF16 = jnp.bfloat16
SHIFTS = (0, 1, 3, 2)


def embed(visible, full_width):
    patch_id = jnp.maximum(visible, 0)
    plane_size = GRID * GRID
    coord_x = (patch_id // plane_size).astype(F32)
    coord_y = (patch_id // GRID % GRID).astype(F32)
    coord_z = (patch_id % GRID).astype(F32)
    channel = jnp.arange(full_width, dtype=jnp.int32)
    axis_pick = channel % 3
    frequency = jnp.exp(-math.log(10000.0) * (channel // 6 * 6).astype(F32) / full_width)
    offset_phase = 0.5 * math.pi * (channel // 3 % 2).astype(F32)
    picked = jnp.where(
        axis_pick[None, :] == 0,
        coord_x[:, None],
        jnp.where(axis_pick[None, :] == 1, coord_y[:, None], coord_z[:, None]),
    )
    return jnp.sin(picked * frequency[None, :] + offset_phase[None, :])


def spread(block, axes, count):
    copies = jnp.broadcast_to(block[None], (count,) + block.shape)
    return lax.all_to_all(copies, axes, 0, 0)


def ring(count, shift):
    return [(i, (i + shift) % count) for i in range(count)]


def norm_kernel(par_ref, near_ref, side_ref, pos_ref, gain_ref, bias_ref, out_ref):
    step = 64
    even = par_ref[0] == 0
    for r in range(0, ROWS, step):
        rows = slice(r, r + step)
        parts = []
        for z in range(8):
            near = near_ref[z // 2, rows, :]
            side = side_ref[z // 2, rows, :]
            mine = jnp.where(even == (z % 2 == 0), near, side)
            parts.append(mine.astype(F32) + pos_ref[rows, z * 256 : (z + 1) * 256])
        total = sum(jnp.sum(p, axis=1, keepdims=True) for p in parts)
        mean = total * (1.0 / 2048)
        parts = [p - mean for p in parts]
        square = sum(jnp.sum(p * p, axis=1, keepdims=True) for p in parts)
        scale = lax.rsqrt(square * (1.0 / 2048) + 1e-06)
        for z in range(8):
            lanes = slice(z * 256, (z + 1) * 256)
            value = parts[z] * scale * gain_ref[:, lanes] + bias_ref[:, lanes]
            out_ref[z // 2, rows, (z % 2) * 256 : (z % 2 + 1) * 256] = value.astype(BF16)


def qkv_kernel(
    src_ref, core_ref, own_ref, oth_ref, w0_ref, w1_ref, w2_ref, w3_ref, cnt_ref, q_ref, kv_ref, kvs_ref
):
    for c, n_ref in enumerate((own_ref, oth_ref)):
        acc = jnp.zeros((ROWS, 384), F32)
        for s, w_ref in enumerate((w0_ref, w1_ref, w2_ref, w3_ref)):
            acc = acc + jnp.dot(n_ref[src_ref[s]], w_ref[:, :384], preferred_element_type=F32)
        at = pl.multiple_of((core_ref[0] ^ c) * ROWS, ROWS)
        query = (acc[:, :128] * (1.0 / math.sqrt(HEAD_DIM))).astype(BF16)
        pair = acc[:, 128:384].astype(BF16)
        count = cnt_ref[c].astype(BF16)
        for copy in range(4):
            q_ref[copy, pl.ds(at, ROWS), :] = query
            kvs_ref[copy, c, :ROWS, :] = pair
            kvs_ref[copy, c, ROWS:, :] = count
        kv_ref[c, :ROWS, :] = pair
        kv_ref[c, ROWS:, :] = count


NT = (((1,), (1,)), ((), ()))
TN = (((0,), (0,)), ((), ()))


def scan_keys(query, kv_ref, s_ref, acc_ref, best, total):
    width = query.shape[0]
    blocks = kv_ref.shape[0]
    before = best

    def first(b, best):
        for c in range(2):
            keys = kv_ref[b, c, :ROWS, :128]
            score = lax.dot_general(keys, query, NT, preferred_element_type=F32)
            row = lax.broadcasted_iota(jnp.int32, (ROWS, width), 0).astype(F32)
            live = kv_ref[b, c, pl.ds(ROWS, 1), :].astype(F32)
            live = jnp.concatenate([live] * (width // 256), axis=1)
            score = jnp.where(row < live, score, -1e30)
            s_ref[pl.ds((b * 2 + c) * ROWS, ROWS), :] = score
            best = jnp.maximum(best, jnp.max(score, axis=0, keepdims=True))
        return best

    best = lax.fori_loop(0, blocks, first, best)
    shrink = jnp.exp(before - best)
    total = total * shrink
    acc_ref[...] = acc_ref[...] * shrink

    def second(b, total):
        for c in range(2):
            weight = jnp.exp(s_ref[pl.ds((b * 2 + c) * ROWS, ROWS), :] - best)
            total = total + jnp.sum(weight, axis=0, keepdims=True)
            values = kv_ref[b, c, :ROWS, 128:256]
            acc_ref[...] += lax.dot_general(
                values, weight.astype(BF16), TN, preferred_element_type=F32
            )
        return total

    return best, lax.fori_loop(0, blocks, second, total)


def near_kernel(q_ref, kv_ref, acc_ref, stat_ref, s_ref):
    width = q_ref.shape[0]
    acc_ref[...] = jnp.zeros_like(acc_ref)
    best, total = scan_keys(
        q_ref[...],
        kv_ref,
        s_ref,
        acc_ref,
        jnp.full((1, width), -1e30, F32),
        jnp.zeros((1, width), F32),
    )
    stat_ref[0:1, :] = best
    stat_ref[1:2, :] = total
    stat_ref[2:8, :] = jnp.zeros((6, width), F32)


def far_kernel(q_ref, kv_ref, part_ref, stat_ref, out_ref, s_ref, acc_ref):
    width = q_ref.shape[0]
    acc_ref[...] = part_ref[...]
    best, total = scan_keys(
        q_ref[...], kv_ref, s_ref, acc_ref, stat_ref[0:1, :], stat_ref[1:2, :]
    )
    mixed = (acc_ref[...] / total).T.astype(BF16)
    level = best + jnp.log(total)
    high = level.astype(BF16)
    rest = level - high.astype(F32)
    mid = rest.astype(BF16)
    low = (rest - mid.astype(F32)).astype(BF16)
    for x in range(width // (2 * ROWS)):
        stats = []
        for part in (high, mid, low):
            for piece in range(3):
                at = x * 2 * ROWS + piece * 128
                stats.append(part[:, at : at + 128].astype(F32))
        stats.append(jnp.zeros((7, 128), F32))
        stats = jnp.concatenate(stats, axis=0).astype(BF16)
        for c in range(2):
            at = (2 * x + c) * ROWS
            out_ref[2 * x + c, :ROWS, :] = mixed[at : at + ROWS, :]
            out_ref[2 * x + c, ROWS : ROWS + 16, :] = stats


def out_kernel(src_ref, par_ref, near_ref, side_ref, w0_ref, w1_ref, w2_ref, w3_ref, out_ref):
    acc = jnp.zeros(out_ref.shape, F32)
    for s, w_ref in enumerate((w0_ref, w1_ref, w2_ref, w3_ref)):
        for flip, m_ref in enumerate((near_ref, side_ref)):
            at = pl.multiple_of((par_ref[0] ^ flip) * 256, 256)
            acc = acc + jnp.dot(
                m_ref[src_ref[s]], w_ref[pl.ds(at, 256), 384:640], preferred_element_type=F32
            )
    out_ref[...] = acc


VMEM = pl.BlockSpec(memory_space=pltpu.VMEM)
SMEM = pl.BlockSpec(memory_space=pltpu.SMEM)
PARAMS = pltpu.CompilerParams(vmem_limit_bytes=20 * 1024 * 1024)


def sublayer(patches, visible, ln_gain, ln_bias, w_query, w_key, w_value, w_output):
    core = lax.axis_index("core")
    row = lax.axis_index("row")
    lane = core * HEAD_DIM
    w_own = jnp.concatenate(
        [lax.dynamic_slice_in_dim(w, lane, HEAD_DIM, 1) for w in (w_query, w_key, w_value)]
        + [w_output],
        axis=1,
    )
    weights = [w_own]
    weights += [lax.ppermute(w_own, "row", ring(4, s)) for s in SHIFTS[1:]]
    source = jnp.stack([(row - s) % 4 for s in SHIFTS]).astype(jnp.int32)
    core = core.astype(jnp.int32)[None]
    parity = lax.axis_index("c0").astype(jnp.int32)[None]

    live = jnp.full((16, 256), jnp.sum((visible >= 0).astype(F32)), F32)
    counts = jnp.stack([live, lax.ppermute(live, "core", ring(2, 1))])

    pos = embed(visible, 2048)
    near = spread(patches, ("c2", "c1"), 4)
    near, weights, counts = lax.optimization_barrier((near, weights, counts))
    side = lax.ppermute(near, "c0", ring(2, 1))
    own = pl.pallas_call(
        norm_kernel,
        out_shape=jax.ShapeDtypeStruct((4, ROWS, 512), BF16),
        in_specs=[SMEM] + [VMEM] * 5,
        out_specs=VMEM,
        compiler_params=PARAMS,
        name="norm",
    )(parity, near, side, pos, ln_gain[None, :], ln_bias[None, :])
    other = lax.ppermute(own, "core", ring(2, 1))
    query, kv, near_kv = pl.pallas_call(
        qkv_kernel,
        out_shape=(
            jax.ShapeDtypeStruct((4, 2 * ROWS, 128), BF16),
            jax.ShapeDtypeStruct((2, ROWS + 16, 256), BF16),
            jax.ShapeDtypeStruct((4, 2, ROWS + 16, 256), BF16),
        ),
        in_specs=[SMEM] * 2 + [VMEM] * 7,
        out_specs=(VMEM, VMEM, VMEM),
        compiler_params=PARAMS,
        name="qkv",
    )(source, core, own, other, *weights, counts)
    far_kv = lax.ppermute(kv, ("zh", "c2", "c1", "c0"), ring(16, 8))
    query = lax.all_to_all(query, "row", 0, 0).reshape(8 * ROWS, 128)
    near_kv = lax.all_to_all(near_kv, "y", 0, 0)
    far_kv, _ = lax.optimization_barrier((far_kv, near_kv))
    far_kv = spread(far_kv, "y", 4)
    kv_spec = pl.BlockSpec((4, 2, ROWS + 16, 256), lambda i: (0, 0, 0, 0))
    q_spec = pl.BlockSpec((4 * ROWS, 128), lambda i: (i, 0))
    acc_spec = pl.BlockSpec((128, 4 * ROWS), lambda i: (0, i))
    stat_spec = pl.BlockSpec((8, 4 * ROWS), lambda i: (0, i))
    acc, stat = pl.pallas_call(
        near_kernel,
        grid=(2,),
        out_shape=(
            jax.ShapeDtypeStruct((128, 8 * ROWS), F32),
            jax.ShapeDtypeStruct((8, 8 * ROWS), F32),
        ),
        in_specs=[q_spec, kv_spec],
        out_specs=(acc_spec, stat_spec),
        scratch_shapes=[pltpu.VMEM((8 * ROWS, 4 * ROWS), F32)],
        compiler_params=PARAMS,
        name="near",
    )(query, near_kv)
    part = pl.pallas_call(
        far_kernel,
        grid=(2,),
        out_shape=jax.ShapeDtypeStruct((8, ROWS + 16, 128), BF16),
        in_specs=[q_spec, kv_spec, acc_spec, stat_spec],
        out_specs=pl.BlockSpec((4, ROWS + 16, 128), lambda i: (i, 0, 0)),
        scratch_shapes=[
            pltpu.VMEM((8 * ROWS, 4 * ROWS), F32),
            pltpu.VMEM((128, 4 * ROWS), F32),
        ],
        compiler_params=PARAMS,
        name="far",
    )(query, far_kv, acc, stat)
    part = lax.all_to_all(part, ("row", "core"), 0, 0).reshape(4, 2, ROWS + 16, 128)
    stats = part[:, :, ROWS : ROWS + 9, :].astype(F32).reshape(4, 2, 3, 2 * ROWS).sum(axis=2)
    stats = lax.dynamic_slice_in_dim(stats, core[0] * ROWS, ROWS, 2)
    share = jnp.exp(stats - jnp.max(stats, axis=0, keepdims=True))
    share = share / jnp.sum(share, axis=0, keepdims=True)
    mixed = jnp.sum(part[:, :, :ROWS, :].astype(F32) * share[..., None], axis=0)
    mixed = jnp.concatenate([mixed[0], mixed[1]], axis=1).astype(BF16)
    near = spread(mixed, ("c2", "c1"), 4)
    side = lax.ppermute(near, "c0", ring(2, 1))
    return pl.pallas_call(
        out_kernel,
        out_shape=jax.ShapeDtypeStruct((ROWS, 256), F32),
        in_specs=[SMEM] * 2 + [VMEM] * 6,
        out_specs=VMEM,
        compiler_params=PARAMS,
        name="out",
    )(source, parity, near, side, *weights)


def solution(mesh):
    fine = Mesh(
        mesh.devices.reshape(4, 2, 2, 4, 2, 2, 2), ("y", "zh", "core", "row", "c2", "c1", "c0")
    )
    tokens = ("y", "zh", "core", "row")
    col = ("c2", "c1", "c0")
    placed = (
        P(tokens, col),
        P(tokens),
        P(),
        P(),
        P("row", col),
        P("row", col),
        P("row", col),
        P("row", col),
    )
    return jax.shard_map(
        sublayer, mesh=fine, in_specs=placed, out_specs=P(tokens, col), check_vma=False
    )
```

```python
import math

import jax
import jax.numpy as jnp
from jax import lax
from jax.experimental import pallas as pl
from jax.experimental.pallas import tpu as pltpu
from jax.sharding import Mesh
from jax.sharding import PartitionSpec as P


HEAD_DIM = 128
GRID = 64
ROWS = 192
F32 = jnp.float32
BF16 = jnp.bfloat16
SHIFTS = (0, 1, 3, 2)


def embed(visible, full_width):
    patch_id = jnp.maximum(visible, 0)
    plane_size = GRID * GRID
    coord_x = (patch_id // plane_size).astype(F32)
    coord_y = (patch_id // GRID % GRID).astype(F32)
    coord_z = (patch_id % GRID).astype(F32)
    channel = jnp.arange(full_width, dtype=jnp.int32)
    axis_pick = channel % 3
    frequency = jnp.exp(-math.log(10000.0) * (channel // 6 * 6).astype(F32) / full_width)
    offset_phase = 0.5 * math.pi * (channel // 3 % 2).astype(F32)
    picked = jnp.where(
        axis_pick[None, :] == 0,
        coord_x[:, None],
        jnp.where(axis_pick[None, :] == 1, coord_y[:, None], coord_z[:, None]),
    )
    return jnp.sin(picked * frequency[None, :] + offset_phase[None, :])


def spread(block, axes, count):
    copies = jnp.broadcast_to(block[None], (count,) + block.shape)
    return lax.all_to_all(copies, axes, 0, 0)


def ring(count, shift):
    return [(i, (i + shift) % count) for i in range(count)]


def norm_kernel(par_ref, near_ref, side_ref, pos_ref, gain_ref, bias_ref, out_ref):
    step = 64
    even = par_ref[0] == 0
    for r in range(0, ROWS, step):
        rows = slice(r, r + step)
        parts = []
        for z in range(8):
            near = near_ref[z // 2, rows, :]
            side = side_ref[z // 2, rows, :]
            mine = jnp.where(even == (z % 2 == 0), near, side)
            parts.append(mine.astype(F32) + pos_ref[rows, z * 256 : (z + 1) * 256])
        total = sum(jnp.sum(p, axis=1, keepdims=True) for p in parts)
        mean = total * (1.0 / 2048)
        parts = [p - mean for p in parts]
        square = sum(jnp.sum(p * p, axis=1, keepdims=True) for p in parts)
        scale = lax.rsqrt(square * (1.0 / 2048) + 1e-06)
        for z in range(8):
            lanes = slice(z * 256, (z + 1) * 256)
            value = parts[z] * scale * gain_ref[:, lanes] + bias_ref[:, lanes]
            out_ref[z // 2, rows, (z % 2) * 256 : (z % 2 + 1) * 256] = value.astype(BF16)


def qkv_kernel(
    src_ref, core_ref, own_ref, oth_ref, w0_ref, w1_ref, w2_ref, w3_ref, cnt_ref, q_ref, kv_ref, kvs_ref
):
    for c, n_ref in enumerate((own_ref, oth_ref)):
        acc = jnp.zeros((ROWS, 384), F32)
        for s, w_ref in enumerate((w0_ref, w1_ref, w2_ref, w3_ref)):
            acc = acc + jnp.dot(n_ref[src_ref[s]], w_ref[...], preferred_element_type=F32)
        at = pl.multiple_of((core_ref[0] ^ c) * ROWS, ROWS)
        query = (acc[:, :128] * (1.0 / math.sqrt(HEAD_DIM))).astype(BF16)
        pair = acc[:, 128:384].astype(BF16)
        count = cnt_ref[c].astype(BF16)
        for copy in range(4):
            q_ref[copy, pl.ds(at, ROWS), :] = query
            kvs_ref[copy, c, :ROWS, :] = pair
            kvs_ref[copy, c, ROWS:, :] = count
        kv_ref[c, :ROWS, :] = pair
        kv_ref[c, ROWS:, :] = count


NT = (((1,), (1,)), ((), ()))
TN = (((0,), (0,)), ((), ()))


def scan_keys(query, kv_ref, s_ref, acc_ref, best, total):
    width = query.shape[0]
    blocks = kv_ref.shape[0]
    before = best

    def first(b, best):
        for c in range(2):
            keys = kv_ref[b, c, :ROWS, :128]
            score = lax.dot_general(keys, query, NT, preferred_element_type=F32)
            row = lax.broadcasted_iota(jnp.int32, (ROWS, width), 0).astype(F32)
            live = kv_ref[b, c, pl.ds(ROWS, 1), :].astype(F32)
            live = jnp.concatenate([live] * (width // 256), axis=1)
            score = jnp.where(row < live, score, -1e30)
            s_ref[pl.ds((b * 2 + c) * ROWS, ROWS), :] = score
            best = jnp.maximum(best, jnp.max(score, axis=0, keepdims=True))
        return best

    best = lax.fori_loop(0, blocks, first, best)
    shrink = jnp.exp(before - best)
    total = total * shrink
    acc_ref[...] = acc_ref[...] * shrink

    def second(b, total):
        for c in range(2):
            weight = jnp.exp(s_ref[pl.ds((b * 2 + c) * ROWS, ROWS), :] - best)
            total = total + jnp.sum(weight, axis=0, keepdims=True)
            values = kv_ref[b, c, :ROWS, 128:256]
            acc_ref[...] += lax.dot_general(
                values, weight.astype(BF16), TN, preferred_element_type=F32
            )
        return total

    return best, lax.fori_loop(0, blocks, second, total)


def near_kernel(q_ref, kv_ref, acc_ref, stat_ref, s_ref):
    width = q_ref.shape[0]
    acc_ref[...] = jnp.zeros_like(acc_ref)
    best, total = scan_keys(
        q_ref[...],
        kv_ref,
        s_ref,
        acc_ref,
        jnp.full((1, width), -1e30, F32),
        jnp.zeros((1, width), F32),
    )
    stat_ref[0:1, :] = best
    stat_ref[1:2, :] = total
    stat_ref[2:8, :] = jnp.zeros((6, width), F32)


def far_kernel(q_ref, kv_ref, part_ref, stat_ref, out_ref, s_ref, acc_ref):
    width = q_ref.shape[0]
    acc_ref[...] = part_ref[...]
    best, total = scan_keys(
        q_ref[...], kv_ref, s_ref, acc_ref, stat_ref[0:1, :], stat_ref[1:2, :]
    )
    mixed = (acc_ref[...] / total).T.astype(BF16)
    level = best + jnp.log(total)
    high = level.astype(BF16)
    rest = level - high.astype(F32)
    mid = rest.astype(BF16)
    low = (rest - mid.astype(F32)).astype(BF16)
    for x in range(width // (2 * ROWS)):
        stats = []
        for part in (high, mid, low):
            for piece in range(3):
                at = x * 2 * ROWS + piece * 128
                stats.append(part[:, at : at + 128].astype(F32))
        stats.append(jnp.zeros((7, 128), F32))
        stats = jnp.concatenate(stats, axis=0).astype(BF16)
        for c in range(2):
            at = (2 * x + c) * ROWS
            out_ref[2 * x + c, :ROWS, :] = mixed[at : at + ROWS, :]
            out_ref[2 * x + c, ROWS : ROWS + 16, :] = stats


def out_kernel(src_ref, half_ref, m_ref, w0_ref, w1_ref, w2_ref, w3_ref, out_ref):
    acc = jnp.zeros(out_ref.shape, F32)
    for s, w_ref in enumerate((w0_ref, w1_ref, w2_ref, w3_ref)):
        for step in range(2):
            at = src_ref[s] + step
            acc = acc + jnp.dot(
                m_ref[at % 4, half_ref[0] ^ (at // 4)],
                w_ref[step * 256 : (step + 1) * 256, :],
                preferred_element_type=F32,
            )
    out_ref[...] = acc


VMEM = pl.BlockSpec(memory_space=pltpu.VMEM)
SMEM = pl.BlockSpec(memory_space=pltpu.SMEM)
PARAMS = pltpu.CompilerParams(vmem_limit_bytes=20 * 1024 * 1024)


def sublayer(patches, visible, ln_gain, ln_bias, w_query, w_key, w_value, w_output):
    core = lax.axis_index("core")
    row = lax.axis_index("row")
    lane = core * HEAD_DIM
    w_own = jnp.concatenate(
        [lax.dynamic_slice_in_dim(w, lane, HEAD_DIM, 1) for w in (w_query, w_key, w_value)],
        axis=1,
    )
    weights = [w_own]
    weights += [lax.ppermute(w_own, "row", ring(4, s)) for s in SHIFTS[1:]]
    outward = [w_output]
    outward += [lax.ppermute(w_output, "row", ring(4, s)) for s in SHIFTS[1:]]
    source = jnp.stack([(row - s) % 4 for s in SHIFTS]).astype(jnp.int32)
    chunks = jnp.stack([(row - s) % 4 * 2 for s in SHIFTS]).astype(jnp.int32)
    core = core.astype(jnp.int32)[None]
    parity = lax.axis_index("c0").astype(jnp.int32)[None]
    half = lax.axis_index("c2").astype(jnp.int32)[None]

    live = jnp.full((16, 256), jnp.sum((visible >= 0).astype(F32)), F32)
    counts = jnp.stack([live, lax.ppermute(live, "core", ring(2, 1))])

    pos = embed(visible, 2048)
    near = spread(patches, ("c2", "c1"), 4)
    near, counts = lax.optimization_barrier((near, counts))
    side = lax.ppermute(near, "c0", ring(2, 1))
    own = pl.pallas_call(
        norm_kernel,
        out_shape=jax.ShapeDtypeStruct((4, ROWS, 512), BF16),
        in_specs=[SMEM] + [VMEM] * 5,
        out_specs=VMEM,
        compiler_params=PARAMS,
        name="norm",
    )(parity, near, side, pos, ln_gain[None, :], ln_bias[None, :])
    other = lax.ppermute(own, "core", ring(2, 1))
    query, kv, near_kv = pl.pallas_call(
        qkv_kernel,
        out_shape=(
            jax.ShapeDtypeStruct((4, 2 * ROWS, 128), BF16),
            jax.ShapeDtypeStruct((2, ROWS + 16, 256), BF16),
            jax.ShapeDtypeStruct((4, 2, ROWS + 16, 256), BF16),
        ),
        in_specs=[SMEM] * 2 + [VMEM] * 7,
        out_specs=(VMEM, VMEM, VMEM),
        compiler_params=PARAMS,
        name="qkv",
    )(source, core, own, other, *weights, counts)
    far_kv = lax.ppermute(kv, ("zh", "c2", "c1", "c0"), ring(16, 8))
    query = lax.all_to_all(query, "row", 0, 0).reshape(8 * ROWS, 128)
    near_kv = lax.all_to_all(near_kv, "y", 0, 0)
    far_kv, _ = lax.optimization_barrier((far_kv, near_kv))
    far_kv = spread(far_kv, "y", 4)
    kv_spec = pl.BlockSpec((4, 2, ROWS + 16, 256), lambda i: (0, 0, 0, 0))
    q_spec = pl.BlockSpec((4 * ROWS, 128), lambda i: (i, 0))
    acc_spec = pl.BlockSpec((128, 4 * ROWS), lambda i: (0, i))
    stat_spec = pl.BlockSpec((8, 4 * ROWS), lambda i: (0, i))
    acc, stat = pl.pallas_call(
        near_kernel,
        grid=(2,),
        out_shape=(
            jax.ShapeDtypeStruct((128, 8 * ROWS), F32),
            jax.ShapeDtypeStruct((8, 8 * ROWS), F32),
        ),
        in_specs=[q_spec, kv_spec],
        out_specs=(acc_spec, stat_spec),
        scratch_shapes=[pltpu.VMEM((8 * ROWS, 4 * ROWS), F32)],
        compiler_params=PARAMS,
        name="near",
    )(query, near_kv)
    part = pl.pallas_call(
        far_kernel,
        grid=(2,),
        out_shape=jax.ShapeDtypeStruct((8, ROWS + 16, 128), BF16),
        in_specs=[q_spec, kv_spec, acc_spec, stat_spec],
        out_specs=pl.BlockSpec((4, ROWS + 16, 128), lambda i: (i, 0, 0)),
        scratch_shapes=[
            pltpu.VMEM((8 * ROWS, 4 * ROWS), F32),
            pltpu.VMEM((128, 4 * ROWS), F32),
        ],
        compiler_params=PARAMS,
        name="far",
    )(query, far_kv, acc, stat)
    part = lax.all_to_all(part, ("row", "core"), 0, 0).reshape(4, 2, ROWS + 16, 128)
    stats = part[:, :, ROWS : ROWS + 9, :].astype(F32).reshape(4, 2, 3, 2 * ROWS).sum(axis=2)
    stats = lax.dynamic_slice_in_dim(stats, core[0] * ROWS, ROWS, 2)
    share = jnp.exp(stats - jnp.max(stats, axis=0, keepdims=True))
    share = share / jnp.sum(share, axis=0, keepdims=True)
    mixed = jnp.sum(part[:, :, :ROWS, :].astype(F32) * share[..., None], axis=0)
    mixed = jnp.concatenate([mixed[0], mixed[1]], axis=1).astype(BF16)
    swapped = lax.ppermute(mixed, "c2", ring(2, 1))
    mixed = jnp.stack([mixed, swapped])
    mixed = spread(mixed, ("c1", "c0"), 4)
    return pl.pallas_call(
        out_kernel,
        out_shape=jax.ShapeDtypeStruct((ROWS, 256), F32),
        in_specs=[SMEM] * 2 + [VMEM] * 5,
        out_specs=VMEM,
        compiler_params=PARAMS,
        name="out",
    )(chunks, half, mixed, *outward)


def solution(mesh):
    fine = Mesh(
        mesh.devices.reshape(4, 2, 2, 4, 2, 2, 2), ("y", "zh", "core", "row", "c2", "c1", "c0")
    )
    tokens = ("y", "zh", "core", "row")
    col = ("c2", "c1", "c0")
    placed = (
        P(tokens, col),
        P(tokens),
        P(),
        P(),
        P("row", col),
        P("row", col),
        P("row", col),
        P("row", col),
    )
    return jax.shard_map(
        sublayer, mesh=fine, in_specs=placed, out_specs=P(tokens, col), check_vma=False
    )
```

```python
import math

import jax
import jax.numpy as jnp
from jax import lax
from jax.experimental import pallas as pl
from jax.experimental.pallas import tpu as pltpu
from jax.sharding import Mesh
from jax.sharding import PartitionSpec as P


HEAD_DIM = 128
GRID = 64
ROWS = 192
F32 = jnp.float32
BF16 = jnp.bfloat16
SHIFTS = (0, 1, 3, 2)


def embed(visible, full_width):
    patch_id = jnp.maximum(visible, 0)
    plane_size = GRID * GRID
    coord_x = (patch_id // plane_size).astype(F32)
    coord_y = (patch_id // GRID % GRID).astype(F32)
    coord_z = (patch_id % GRID).astype(F32)
    channel = jnp.arange(full_width, dtype=jnp.int32)
    axis_pick = channel % 3
    frequency = jnp.exp(-math.log(10000.0) * (channel // 6 * 6).astype(F32) / full_width)
    offset_phase = 0.5 * math.pi * (channel // 3 % 2).astype(F32)
    picked = jnp.where(
        axis_pick[None, :] == 0,
        coord_x[:, None],
        jnp.where(axis_pick[None, :] == 1, coord_y[:, None], coord_z[:, None]),
    )
    return jnp.sin(picked * frequency[None, :] + offset_phase[None, :])


def spread(block, axes, count):
    copies = jnp.broadcast_to(block[None], (count,) + block.shape)
    return lax.all_to_all(copies, axes, 0, 0)


def ring(count, shift):
    return [(i, (i + shift) % count) for i in range(count)]


def norm_kernel(par_ref, near_ref, side_ref, pos_ref, gain_ref, bias_ref, out_ref):
    step = 64
    even = par_ref[0] == 0
    for r in range(0, ROWS, step):
        rows = slice(r, r + step)
        parts = []
        for z in range(8):
            near = near_ref[z // 2, rows, :]
            side = side_ref[z // 2, rows, :]
            mine = jnp.where(even == (z % 2 == 0), near, side)
            parts.append(mine.astype(F32) + pos_ref[rows, z * 256 : (z + 1) * 256])
        total = sum(jnp.sum(p, axis=1, keepdims=True) for p in parts)
        mean = total * (1.0 / 2048)
        parts = [p - mean for p in parts]
        square = sum(jnp.sum(p * p, axis=1, keepdims=True) for p in parts)
        scale = lax.rsqrt(square * (1.0 / 2048) + 1e-06)
        for z in range(8):
            lanes = slice(z * 256, (z + 1) * 256)
            value = parts[z] * scale * gain_ref[:, lanes] + bias_ref[:, lanes]
            out_ref[z // 2, rows, (z % 2) * 256 : (z % 2 + 1) * 256] = value.astype(BF16)


def qkv_kernel(
    src_ref, core_ref, own_ref, oth_ref, w0_ref, w1_ref, w2_ref, w3_ref, cnt_ref, q_ref, kv_ref
):
    for c, n_ref in enumerate((own_ref, oth_ref)):
        acc = jnp.zeros((ROWS, 384), F32)
        for s, w_ref in enumerate((w0_ref, w1_ref, w2_ref, w3_ref)):
            acc = acc + jnp.dot(n_ref[src_ref[s]], w_ref[...], preferred_element_type=F32)
        at = pl.multiple_of((core_ref[0] ^ c) * ROWS, ROWS)
        query = (acc[:, :128] * (1.0 / math.sqrt(HEAD_DIM))).astype(BF16)
        pair = acc[:, 128:384].astype(BF16)
        count = cnt_ref[c].astype(BF16)
        for copy in range(4):
            q_ref[copy, pl.ds(at, ROWS), :] = query
        kv_ref[c, :ROWS, :] = pair
        kv_ref[c, ROWS:, :] = count


NT = (((1,), (1,)), ((), ()))
TN = (((0,), (0,)), ((), ()))


def scan_keys(query, kv_refs, s_ref, acc_ref, best, total):
    width = query.shape[0]
    before = best

    def over(body, carry):
        base = 0
        for kv_ref in kv_refs:
            for b in range(kv_ref.shape[0]):
                carry = body(kv_ref, b, base + b, carry)
            base += kv_ref.shape[0]
        return carry

    def first(kv_ref, b, at, best):
        for c in range(2):
            keys = kv_ref[b, c, :ROWS, :128]
            score = lax.dot_general(keys, query, NT, preferred_element_type=F32)
            row = lax.broadcasted_iota(jnp.int32, (ROWS, width), 0).astype(F32)
            live = kv_ref[b, c, pl.ds(ROWS, 1), :].astype(F32)
            live = jnp.concatenate([live] * (width // 256), axis=1)
            score = jnp.where(row < live, score, -1e30)
            s_ref[pl.ds((at * 2 + c) * ROWS, ROWS), :] = score
            best = jnp.maximum(best, jnp.max(score, axis=0, keepdims=True))
        return best

    best = over(first, best)
    shrink = jnp.exp(before - best)
    total = total * shrink
    acc_ref[...] = acc_ref[...] * shrink

    def second(kv_ref, b, at, total):
        for c in range(2):
            weight = jnp.exp(s_ref[pl.ds((at * 2 + c) * ROWS, ROWS), :] - best)
            total = total + jnp.sum(weight, axis=0, keepdims=True)
            values = kv_ref[b, c, :ROWS, 128:256]
            acc_ref[...] += lax.dot_general(
                values, weight.astype(BF16), TN, preferred_element_type=F32
            )
        return total

    return best, over(second, total)


def near_kernel(q_ref, k0_ref, k1_ref, k2_ref, k3_ref, acc_ref, stat_ref, s_ref):
    width = q_ref.shape[0]
    acc_ref[...] = jnp.zeros_like(acc_ref)
    best, total = scan_keys(
        q_ref[...],
        (k0_ref, k1_ref, k2_ref, k3_ref),
        s_ref,
        acc_ref,
        jnp.full((1, width), -1e30, F32),
        jnp.zeros((1, width), F32),
    )
    stat_ref[0:1, :] = best
    stat_ref[1:2, :] = total
    stat_ref[2:8, :] = jnp.zeros((6, width), F32)


def far_kernel(q_ref, kv_ref, part_ref, stat_ref, out_ref, s_ref, acc_ref):
    width = q_ref.shape[0]
    acc_ref[...] = part_ref[...]
    best, total = scan_keys(
        q_ref[...], (kv_ref,), s_ref, acc_ref, stat_ref[0:1, :], stat_ref[1:2, :]
    )
    mixed = (acc_ref[...] / total).T.astype(BF16)
    level = best + jnp.log(total)
    high = level.astype(BF16)
    rest = level - high.astype(F32)
    mid = rest.astype(BF16)
    low = (rest - mid.astype(F32)).astype(BF16)
    for x in range(width // (2 * ROWS)):
        stats = []
        for part in (high, mid, low):
            for piece in range(3):
                at = x * 2 * ROWS + piece * 128
                stats.append(part[:, at : at + 128].astype(F32))
        stats.append(jnp.zeros((7, 128), F32))
        stats = jnp.concatenate(stats, axis=0).astype(BF16)
        for c in range(2):
            at = (2 * x + c) * ROWS
            out_ref[2 * x + c, :ROWS, :] = mixed[at : at + ROWS, :]
            out_ref[2 * x + c, ROWS : ROWS + 16, :] = stats


def out_kernel(
    src_ref, grp_ref, m0_ref, m1_ref, m2_ref, m3_ref, w0_ref, w1_ref, w2_ref, w3_ref, own_ref, away_ref, w_ref
):
    for s, piece_ref in enumerate((w0_ref, w1_ref, w2_ref, w3_ref)):
        w_ref[src_ref[s]] = piece_ref[...]
    acc = jnp.zeros((ROWS, 512), F32)
    for k, m_ref in enumerate((m0_ref, m1_ref, m2_ref, m3_ref)):
        acc = acc + jnp.dot(m_ref[...], w_ref[grp_ref[k]], preferred_element_type=F32)
    own_ref[...] = acc[:, :256]
    away_ref[...] = acc[:, 256:].astype(BF16)


VMEM = pl.BlockSpec(memory_space=pltpu.VMEM)
SMEM = pl.BlockSpec(memory_space=pltpu.SMEM)
PARAMS = pltpu.CompilerParams(vmem_limit_bytes=20 * 1024 * 1024)


def sublayer(patches, visible, ln_gain, ln_bias, w_query, w_key, w_value, w_output):
    core = lax.axis_index("core")
    row = lax.axis_index("row")
    lane = core * HEAD_DIM
    w_own = jnp.concatenate(
        [lax.dynamic_slice_in_dim(w, lane, HEAD_DIM, 1) for w in (w_query, w_key, w_value)],
        axis=1,
    )
    weights = [w_own]
    weights += [lax.ppermute(w_own, "row", ring(4, s)) for s in SHIFTS[1:]]
    source = jnp.stack([(row - s) % 4 for s in SHIFTS]).astype(jnp.int32)
    place = lax.axis_index(("c2", "c1"))
    group = jnp.stack([place ^ (k % 4) for k in range(8)]).astype(jnp.int32)
    chunks = jnp.stack([(row - s + 8) % 4 for s in SHIFTS]).astype(jnp.int32)
    core = core.astype(jnp.int32)[None]
    parity = lax.axis_index("c0").astype(jnp.int32)[None]

    live = jnp.full((16, 256), jnp.sum((visible >= 0).astype(F32)), F32)
    counts = jnp.stack([live, lax.ppermute(live, "core", ring(2, 1))])

    pos = embed(visible, 2048)
    near = spread(patches, ("c2", "c1"), 4)
    near, counts = lax.optimization_barrier((near, counts))
    side = lax.ppermute(near, "c0", ring(2, 1))
    keep = lax.dynamic_slice_in_dim(w_output, parity[0] * 256, 256, 0)
    give = lax.dynamic_slice_in_dim(w_output, (1 - parity[0]) * 256, 256, 0)
    taken = lax.ppermute(give, "c0", ring(2, 1))
    own = pl.pallas_call(
        norm_kernel,
        out_shape=jax.ShapeDtypeStruct((4, ROWS, 512), BF16),
        in_specs=[SMEM] + [VMEM] * 5,
        out_specs=VMEM,
        compiler_params=PARAMS,
        name="norm",
    )(parity, near, side, pos, ln_gain[None, :], ln_bias[None, :])
    other = lax.ppermute(own, "core", ring(2, 1))
    query, kv = pl.pallas_call(
        qkv_kernel,
        out_shape=(
            jax.ShapeDtypeStruct((4, 2 * ROWS, 128), BF16),
            jax.ShapeDtypeStruct((2, ROWS + 16, 256), BF16),
        ),
        in_specs=[SMEM] * 2 + [VMEM] * 7,
        out_specs=(VMEM, VMEM),
        compiler_params=PARAMS,
        name="qkv",
    )(source, core, own, other, *weights, counts)
    far_kv = lax.ppermute(kv, ("zh", "c2", "c1", "c0"), ring(16, 8))
    query = lax.all_to_all(query, "row", 0, 0).reshape(8 * ROWS, 128)
    near_kv = [kv[None]]
    near_kv += [lax.ppermute(kv, "y", ring(4, s))[None] for s in SHIFTS[1:]]
    far_kv = spread(far_kv, "y", 4)
    kv_spec = pl.BlockSpec((4, 2, ROWS + 16, 256), lambda i: (0, 0, 0, 0))
    one_spec = pl.BlockSpec((1, 2, ROWS + 16, 256), lambda i: (0, 0, 0, 0))
    q_spec = pl.BlockSpec((4 * ROWS, 128), lambda i: (i, 0))
    acc_spec = pl.BlockSpec((128, 4 * ROWS), lambda i: (0, i))
    stat_spec = pl.BlockSpec((8, 4 * ROWS), lambda i: (0, i))
    acc, stat = pl.pallas_call(
        near_kernel,
        grid=(2,),
        out_shape=(
            jax.ShapeDtypeStruct((128, 8 * ROWS), F32),
            jax.ShapeDtypeStruct((8, 8 * ROWS), F32),
        ),
        in_specs=[q_spec] + [one_spec] * 4,
        out_specs=(acc_spec, stat_spec),
        scratch_shapes=[pltpu.VMEM((8 * ROWS, 4 * ROWS), F32)],
        compiler_params=PARAMS,
        name="near",
    )(query, *near_kv)
    part = pl.pallas_call(
        far_kernel,
        grid=(2,),
        out_shape=jax.ShapeDtypeStruct((8, ROWS + 16, 128), BF16),
        in_specs=[q_spec, kv_spec, acc_spec, stat_spec],
        out_specs=pl.BlockSpec((4, ROWS + 16, 128), lambda i: (i, 0, 0)),
        scratch_shapes=[
            pltpu.VMEM((8 * ROWS, 4 * ROWS), F32),
            pltpu.VMEM((128, 4 * ROWS), F32),
        ],
        compiler_params=PARAMS,
        name="far",
    )(query, far_kv, acc, stat)
    outward = [jnp.concatenate([keep, taken], axis=1)]
    outward += [lax.ppermute(outward[0], "row", ring(4, s)) for s in SHIFTS[1:3]]
    outward.append(lax.ppermute(outward[0], "row", ring(4, SHIFTS[3])))
    part = lax.all_to_all(part, ("row", "core"), 0, 0).reshape(4, 2, ROWS + 16, 128)
    stats = part[:, :, ROWS : ROWS + 9, :].astype(F32).reshape(4, 2, 3, 2 * ROWS).sum(axis=2)
    stats = lax.dynamic_slice_in_dim(stats, core[0] * ROWS, ROWS, 2)
    share = jnp.exp(stats - jnp.max(stats, axis=0, keepdims=True))
    share = share / jnp.sum(share, axis=0, keepdims=True)
    mixed = jnp.sum(part[:, :, :ROWS, :].astype(F32) * share[..., None], axis=0)
    mixed = jnp.concatenate([mixed[0], mixed[1]], axis=1).astype(BF16)
    heads = [mixed]
    for k in (1, 2, 3):
        pairs = [(g, g ^ k) for g in range(4)]
        heads.append(lax.ppermute(mixed, ("c2", "c1"), pairs))
    own, away = pl.pallas_call(
        out_kernel,
        out_shape=(
            jax.ShapeDtypeStruct((ROWS, 256), F32),
            jax.ShapeDtypeStruct((ROWS, 256), BF16),
        ),
        in_specs=[SMEM] * 2 + [VMEM] * 8,
        out_specs=(VMEM, VMEM),
        scratch_shapes=[pltpu.VMEM((4, 256, 512), BF16)],
        compiler_params=PARAMS,
        name="out",
    )(chunks, group, *heads, *outward)
    return own + lax.ppermute(away, "c0", ring(2, 1)).astype(F32)


def solution(mesh):
    fine = Mesh(
        mesh.devices.reshape(4, 2, 2, 4, 2, 2, 2), ("y", "zh", "core", "row", "c2", "c1", "c0")
    )
    tokens = ("y", "zh", "core", "row")
    col = ("c2", "c1", "c0")
    placed = (
        P(tokens, col),
        P(tokens),
        P(),
        P(),
        P("row", col),
        P("row", col),
        P("row", col),
        P("row", col),
    )
    return jax.shard_map(
        sublayer, mesh=fine, in_specs=placed, out_specs=P(tokens, col), check_vma=False
    )
```

```python
import math

import jax
import jax.numpy as jnp
from jax import lax
from jax.experimental import pallas as pl
from jax.experimental.pallas import tpu as pltpu
from jax.sharding import Mesh
from jax.sharding import PartitionSpec as P


HEAD_DIM = 128
GRID = 64
ROWS = 192
F32 = jnp.float32
BF16 = jnp.bfloat16
SHIFTS = (0, 1, 3, 2)


def embed(visible, full_width):
    patch_id = jnp.maximum(visible, 0)
    plane_size = GRID * GRID
    coord_x = (patch_id // plane_size).astype(F32)
    coord_y = (patch_id // GRID % GRID).astype(F32)
    coord_z = (patch_id % GRID).astype(F32)
    channel = jnp.arange(full_width, dtype=jnp.int32)
    axis_pick = channel % 3
    frequency = jnp.exp(-math.log(10000.0) * (channel // 6 * 6).astype(F32) / full_width)
    offset_phase = 0.5 * math.pi * (channel // 3 % 2).astype(F32)
    picked = jnp.where(
        axis_pick[None, :] == 0,
        coord_x[:, None],
        jnp.where(axis_pick[None, :] == 1, coord_y[:, None], coord_z[:, None]),
    )
    return jnp.sin(picked * frequency[None, :] + offset_phase[None, :])


def spread(block, axes, count):
    copies = jnp.broadcast_to(block[None], (count,) + block.shape)
    return lax.all_to_all(copies, axes, 0, 0)


def ring(count, shift):
    return [(i, (i + shift) % count) for i in range(count)]


def norm_kernel(par_ref, near_ref, side_ref, pos_ref, gain_ref, bias_ref, out_ref):
    step = 64
    even = par_ref[0] == 0
    for r in range(0, ROWS, step):
        rows = slice(r, r + step)
        parts = []
        for z in range(8):
            near = near_ref[z // 2, rows, :]
            side = side_ref[z // 2, rows, :]
            mine = jnp.where(even == (z % 2 == 0), near, side)
            parts.append(mine.astype(F32) + pos_ref[rows, z * 256 : (z + 1) * 256])
        total = sum(jnp.sum(p, axis=1, keepdims=True) for p in parts)
        mean = total * (1.0 / 2048)
        parts = [p - mean for p in parts]
        square = sum(jnp.sum(p * p, axis=1, keepdims=True) for p in parts)
        scale = lax.rsqrt(square * (1.0 / 2048) + 1e-06)
        for z in range(8):
            lanes = slice(z * 256, (z + 1) * 256)
            value = parts[z] * scale * gain_ref[:, lanes] + bias_ref[:, lanes]
            out_ref[z // 2, rows, (z % 2) * 256 : (z % 2 + 1) * 256] = value.astype(BF16)


def qkv_kernel(
    src_ref, core_ref, own_ref, oth_ref, w0_ref, w1_ref, w2_ref, w3_ref, cnt_ref, q_ref, kv_ref
):
    for c, n_ref in enumerate((own_ref, oth_ref)):
        acc = jnp.zeros((ROWS, 384), F32)
        for s, w_ref in enumerate((w0_ref, w1_ref, w2_ref, w3_ref)):
            acc = acc + jnp.dot(n_ref[src_ref[s]], w_ref[...], preferred_element_type=F32)
        at = pl.multiple_of((core_ref[0] ^ c) * ROWS, ROWS)
        query = (acc[:, :128] * (1.0 / math.sqrt(HEAD_DIM))).astype(BF16)
        pair = acc[:, 128:384].astype(BF16)
        count = cnt_ref[c].astype(BF16)
        for copy in range(4):
            q_ref[copy, pl.ds(at, ROWS), :] = query
        kv_ref[c, :ROWS, :] = pair
        kv_ref[c, ROWS:, :] = count


NT = (((1,), (1,)), ((), ()))
TN = (((0,), (0,)), ((), ()))


def scan_keys(query, kv_refs, s_ref, acc_ref, best, total):
    width = query.shape[0]
    before = best

    def over(body, carry):
        base = 0
        for kv_ref in kv_refs:
            for b in range(kv_ref.shape[0]):
                carry = body(kv_ref, b, base + b, carry)
            base += kv_ref.shape[0]
        return carry

    def first(kv_ref, b, at, best):
        for c in range(2):
            keys = kv_ref[b, c, :ROWS, :128]
            score = lax.dot_general(keys, query, NT, preferred_element_type=F32)
            row = lax.broadcasted_iota(jnp.int32, (ROWS, width), 0).astype(F32)
            live = kv_ref[b, c, pl.ds(ROWS, 1), :].astype(F32)
            live = jnp.concatenate([live] * (width // 256), axis=1)
            score = jnp.where(row < live, score, -1e30)
            s_ref[pl.ds((at * 2 + c) * ROWS, ROWS), :] = score
            best = jnp.maximum(best, jnp.max(score, axis=0, keepdims=True))
        return best

    best = over(first, best)
    shrink = jnp.exp(before - best)
    total = total * shrink
    acc_ref[...] = acc_ref[...] * shrink

    def second(kv_ref, b, at, total):
        for c in range(2):
            weight = jnp.exp(s_ref[pl.ds((at * 2 + c) * ROWS, ROWS), :] - best)
            total = total + jnp.sum(weight, axis=0, keepdims=True)
            values = kv_ref[b, c, :ROWS, 128:256]
            acc_ref[...] += lax.dot_general(
                values, weight.astype(BF16), TN, preferred_element_type=F32
            )
        return total

    return best, over(second, total)


def near_kernel(q_ref, k0_ref, k1_ref, acc_ref, stat_ref, s_ref):
    width = s_ref.shape[1]

    def part(i, carry):
        acc_ref[i] = jnp.zeros(acc_ref.shape[1:], F32)
        best, total = scan_keys(
            q_ref[pl.ds(pl.multiple_of(i * width, width), width), :],
            (k0_ref, k1_ref),
            s_ref,
            acc_ref.at[i],
            jnp.full((1, width), -1e30, F32),
            jnp.zeros((1, width), F32),
        )
        stat_ref[i, 0:1, :] = best
        stat_ref[i, 1:2, :] = total
        stat_ref[i, 2:8, :] = jnp.zeros((6, width), F32)
        return carry

    lax.fori_loop(0, 2, part, 0)


def far_kernel(q_ref, kv_ref, part_ref, stat_ref, out_ref, s_ref, acc_ref):
    width = s_ref.shape[1]

    def part(i, carry):
        acc_ref[...] = part_ref[i]
        best, total = scan_keys(
            q_ref[pl.ds(pl.multiple_of(i * width, width), width), :],
            (kv_ref,),
            s_ref,
            acc_ref,
            stat_ref[i, 0:1, :],
            stat_ref[i, 1:2, :],
        )
        mixed = (acc_ref[...] * (1.0 / total)).astype(BF16).T
        level = best + jnp.log(total)
        high = level.astype(BF16)
        rest = level - high.astype(F32)
        mid = rest.astype(BF16)
        low = (rest - mid.astype(F32)).astype(BF16)
        for x in range(width // (2 * ROWS)):
            stats = []
            for piece in (high, mid, low):
                for third in range(3):
                    at = x * 2 * ROWS + third * 128
                    stats.append(piece[:, at : at + 128].astype(F32))
            stats.append(jnp.zeros((7, 128), F32))
            stats = jnp.concatenate(stats, axis=0).astype(BF16)
            for c in range(2):
                at = (2 * x + c) * ROWS
                out_ref[i, 2 * x + c, :ROWS, :] = mixed[at : at + ROWS, :]
                out_ref[i, 2 * x + c, ROWS : ROWS + 16, :] = stats
        return carry

    lax.fori_loop(0, 2, part, 0)


def out_kernel(
    src_ref, grp_ref, m0_ref, m1_ref, m2_ref, m3_ref, w0_ref, w1_ref, w2_ref, w3_ref, own_ref, away_ref, w_ref
):
    for s, piece_ref in enumerate((w0_ref, w1_ref, w2_ref, w3_ref)):
        w_ref[src_ref[s]] = piece_ref[...]
    acc = jnp.zeros((ROWS, 512), F32)
    for k, m_ref in enumerate((m0_ref, m1_ref, m2_ref, m3_ref)):
        acc = acc + jnp.dot(m_ref[...], w_ref[grp_ref[k]], preferred_element_type=F32)
    own_ref[...] = acc[:, :256]
    away_ref[...] = acc[:, 256:].astype(BF16)


VMEM = pl.BlockSpec(memory_space=pltpu.VMEM)
SMEM = pl.BlockSpec(memory_space=pltpu.SMEM)
PARAMS = pltpu.CompilerParams(vmem_limit_bytes=20 * 1024 * 1024)


def sublayer(patches, visible, ln_gain, ln_bias, w_query, w_key, w_value, w_output):
    core = lax.axis_index("core")
    row = lax.axis_index("row")
    lane = core * HEAD_DIM
    w_own = jnp.concatenate(
        [lax.dynamic_slice_in_dim(w, lane, HEAD_DIM, 1) for w in (w_query, w_key, w_value)],
        axis=1,
    )
    weights = [w_own]
    weights += [lax.ppermute(w_own, "row", ring(4, s)) for s in SHIFTS[1:]]
    source = jnp.stack([(row - s) % 4 for s in SHIFTS]).astype(jnp.int32)
    place = lax.axis_index(("c2", "c1"))
    group = jnp.stack([place ^ (k % 4) for k in range(8)]).astype(jnp.int32)
    chunks = jnp.stack([(row - s + 8) % 4 for s in SHIFTS]).astype(jnp.int32)
    core = core.astype(jnp.int32)[None]
    parity = lax.axis_index("c0").astype(jnp.int32)[None]

    live = jnp.full((8, 256), jnp.sum((visible >= 0).astype(F32)), F32)
    counts = jnp.stack([live, lax.ppermute(live, "core", ring(2, 1))])

    pos = embed(visible, 2048)
    near = spread(patches, ("c2", "c1"), 4)
    near, counts = lax.optimization_barrier((near, counts))
    side = lax.ppermute(near, "c0", ring(2, 1))
    keep = lax.dynamic_slice_in_dim(w_output, parity[0] * 256, 256, 0)
    give = lax.dynamic_slice_in_dim(w_output, (1 - parity[0]) * 256, 256, 0)
    taken = lax.ppermute(give, "c0", ring(2, 1))
    own = pl.pallas_call(
        norm_kernel,
        out_shape=jax.ShapeDtypeStruct((4, ROWS, 512), BF16),
        in_specs=[SMEM] + [VMEM] * 5,
        out_specs=VMEM,
        compiler_params=PARAMS,
        name="norm",
    )(parity, near, side, pos, ln_gain[None, :], ln_bias[None, :])
    other = lax.ppermute(own, "core", ring(2, 1))
    query, kv = pl.pallas_call(
        qkv_kernel,
        out_shape=(
            jax.ShapeDtypeStruct((4, 2 * ROWS, 128), BF16),
            jax.ShapeDtypeStruct((2, ROWS + 8, 256), BF16),
        ),
        in_specs=[SMEM] * 2 + [VMEM] * 7,
        out_specs=(VMEM, VMEM),
        compiler_params=PARAMS,
        name="qkv",
    )(source, core, own, other, *weights, counts)
    far_kv = lax.ppermute(kv, ("zh", "c2", "c1", "c0"), ring(16, 8))
    query = lax.all_to_all(query, "row", 0, 0).reshape(8 * ROWS, 128)
    beside = lax.ppermute(kv, "y", [(i, i ^ 1) for i in range(4)])
    near_kv = jnp.stack([kv, beside])
    across = lax.ppermute(near_kv, "y", [(i, i ^ 2) for i in range(4)])
    near_kv = [near_kv, across]
    far_kv = spread(far_kv, "y", 4)
    acc, stat = pl.pallas_call(
        near_kernel,
        out_shape=(
            jax.ShapeDtypeStruct((2, 128, 4 * ROWS), F32),
            jax.ShapeDtypeStruct((2, 8, 4 * ROWS), F32),
        ),
        in_specs=[VMEM] * 3,
        out_specs=(VMEM, VMEM),
        scratch_shapes=[pltpu.VMEM((8 * ROWS, 4 * ROWS), F32)],
        compiler_params=PARAMS,
        name="near",
    )(query, *near_kv)
    part = pl.pallas_call(
        far_kernel,
        out_shape=jax.ShapeDtypeStruct((2, 4, ROWS + 16, 128), BF16),
        in_specs=[VMEM] * 4,
        out_specs=VMEM,
        scratch_shapes=[
            pltpu.VMEM((8 * ROWS, 4 * ROWS), F32),
            pltpu.VMEM((128, 4 * ROWS), F32),
        ],
        compiler_params=PARAMS,
        name="far",
    )(query, far_kv, acc, stat)
    part = part.reshape(8, ROWS + 16, 128)
    outward = [jnp.concatenate([keep, taken], axis=1)]
    outward += [lax.ppermute(outward[0], "row", ring(4, s)) for s in SHIFTS[1:3]]
    outward.append(lax.ppermute(outward[0], "row", ring(4, SHIFTS[3])))
    part = lax.all_to_all(part, ("row", "core"), 0, 0).reshape(4, 2, ROWS + 16, 128)
    stats = part[:, :, ROWS : ROWS + 9, :].astype(F32).reshape(4, 2, 3, 2 * ROWS).sum(axis=2)
    stats = lax.dynamic_slice_in_dim(stats, core[0] * ROWS, ROWS, 2)
    share = jnp.exp(stats - jnp.max(stats, axis=0, keepdims=True))
    share = share / jnp.sum(share, axis=0, keepdims=True)
    mixed = jnp.sum(part[:, :, :ROWS, :].astype(F32) * share[..., None], axis=0)
    mixed = jnp.concatenate([mixed[0], mixed[1]], axis=1).astype(BF16)
    heads = [mixed] + [None] * 3
    for k in (3, 2, 1):
        heads[k] = lax.ppermute(mixed, ("c2", "c1"), [(g, g ^ k) for g in range(4)])
    own, away = pl.pallas_call(
        out_kernel,
        out_shape=(
            jax.ShapeDtypeStruct((ROWS, 256), F32),
            jax.ShapeDtypeStruct((ROWS, 256), BF16),
        ),
        in_specs=[SMEM] * 2 + [VMEM] * 8,
        out_specs=(VMEM, VMEM),
        scratch_shapes=[pltpu.VMEM((4, 256, 512), BF16)],
        compiler_params=PARAMS,
        name="out",
    )(chunks, group, *heads, *outward)
    return own + lax.ppermute(away, "c0", ring(2, 1)).astype(F32)


def solution(mesh):
    fine = Mesh(
        mesh.devices.reshape(4, 2, 2, 4, 2, 2, 2), ("y", "zh", "core", "row", "c2", "c1", "c0")
    )
    tokens = ("y", "zh", "core", "row")
    col = ("c2", "c1", "c0")
    placed = (
        P(tokens, col),
        P(tokens),
        P(),
        P(),
        P("row", col),
        P("row", col),
        P("row", col),
        P("row", col),
    )
    return jax.shard_map(
        sublayer, mesh=fine, in_specs=placed, out_specs=P(tokens, col), check_vma=False
    )
```
